1024 devices in a mesh: ctx: 64 (over x, z), head: 16 (over y, core).
Axes of the slice: x: 8, y: 8, z: 8, core: 2. Of those that a mesh axis runs over, the one named last changes fastest.
Arguments:
- queries: bfloat16 [8192, 6144], P('ctx', 'head'), as said below
- key_rows: bfloat16 [8192, 6144], P('ctx', 'head')
- value_rows: bfloat16 [8192, 6144], P('ctx', 'head'), may hold values from -6 to 6
- summary_index: int32 [64], P('ctx'), may hold values from 0 to 15
- out_weight: bfloat16 [6144, 6144], P('head'), may hold values from -0.078125 to 0.078125
- out_grad: bfloat16 [8192, 6144], P('ctx'), may hold values from -6 to 6
Outputs:
- attended: bfloat16 [8192, 6144], P('ctx', 'head')
- grad_query: bfloat16 [8192, 6144], P('ctx', 'head')
- grad_key: bfloat16 [8192, 6144], P('ctx', 'head')
- grad_value: bfloat16 [8192, 6144], P('ctx', 'head')
The draws below stay inside these ranges and needn't reach their ends.
Inputs may be any that keep to these rules, and one draw needn't show every extreme that they name: queries and keys are finite bfloat16 values.
All inputs are finite; a program needn't handle non-finite values.
Results may differ from the reference program's by a relative error of at most 0.018.
Values may be sent and summed in bfloat16 or wider, within the bound.
A program may use at most 32 MiB of HBM per device.

```python
import jax
import jax.numpy as jnp
from jax import lax

D = 6144
HEADS = 48
HEAD_DIM = 128
STRIDE = 128
SUMMARY = 8
TOKENS = 8192
STRIDES = 64
N_HEAD = 16


def summary_draw(key):
    blocks = STRIDE // SUMMARY
    drawn = jax.random.randint(jax.random.fold_in(key, 15), (STRIDES,), 0, blocks, jnp.int32)
    order = jax.random.permutation(jax.random.fold_in(key, 16), STRIDES)
    drawn = drawn.at[order[0]].set(blocks - 1)
    drawn = drawn.at[order[1]].set(0)
    return drawn


def joint_draw(key):
    width = HEADS * HEAD_DIM
    keys_base = jnp.clip(jax.random.normal(jax.random.fold_in(key, 11), (TOKENS, width), jnp.float32), -6.0, 6.0)
    query_base = jnp.clip(jax.random.normal(jax.random.fold_in(key, 12), (TOKENS, width), jnp.float32), -6.0, 6.0)
    return (query_base, keys_base)


def draw_queries(key, part):
    return joint_draw(key)[0].astype(jnp.bfloat16)


def draw_key_rows(key, part):
    return joint_draw(key)[1].astype(jnp.bfloat16)


def draw_summary_index(key, part):
    return summary_draw(key)


def steps_of(stream_key, shape, split, least, top_value):
    def one(dim, shards_of):
        steps = jax.random.uniform(jax.random.fold_in(jax.random.fold_in(stream_key, 6), dim), (shards_of,), jnp.float32, least / len(split), top_value / len(split))
        return jnp.repeat(jnp.exp(steps), shape[dim] // shards_of).reshape((-1,) + (1,) * (len(shape) - dim - 1))

    loudness = one(*split[0])
    for cut in split[1:]:
        loudness = loudness * one(*cut)
    return loudness


def normal_values(key, extent, deviation, most, shards=(), held_as=jnp.bfloat16):
    loudness = steps_of(key, extent, shards, -0.22, 0.18) if shards else 1.0
    result = jax.random.normal(key, extent, jnp.float32) * deviation * loudness
    return jnp.minimum(jnp.maximum(result, -most), most).astype(held_as)


def setup_inputs(seed: int = 0) -> dict:
    splits = jax.random.split(jax.random.key(seed), 7)
    queries = draw_queries(jax.random.fold_in(splits[6], 71), 0)
    key_rows = draw_key_rows(jax.random.fold_in(splits[6], 71), 0)
    value_rows = normal_values(splits[2], (TOKENS, HEADS * HEAD_DIM), 1.0, 6.0, ((0, 64), (1, 16)))
    summary_index = draw_summary_index(jax.random.fold_in(splits[6], 71), 0)
    out_weight = normal_values(splits[4], (HEADS * HEAD_DIM, D), (HEADS * HEAD_DIM) ** -0.5, 0.078125, ((0, 16),))
    out_grad = normal_values(splits[5], (TOKENS, D), 1.0, 6.0, ((0, 64),))
    return dict(queries=queries, key_rows=key_rows, value_rows=value_rows, summary_index=summary_index, out_weight=out_weight, out_grad=out_grad)


def pick_rows(rows, summary_index):
    blocks = STRIDE // SUMMARY
    width = HEADS * HEAD_DIM
    shaped = rows.reshape(STRIDES, blocks, SUMMARY, width)
    chosen = jnp.take_along_axis(shaped, summary_index.astype(jnp.int32).reshape(STRIDES, 1, 1, 1), axis=1)
    return chosen.reshape(STRIDES * SUMMARY, HEADS, HEAD_DIM)


def reference(queries, key_rows, value_rows, summary_index, out_weight, out_grad):
    scale = HEAD_DIM ** -0.5
    width = HEADS * HEAD_DIM
    blocks = STRIDE // SUMMARY
    slots = STRIDES * SUMMARY
    sum_keys = pick_rows(key_rows, summary_index).astype(jnp.float32)
    sum_vals = pick_rows(value_rows, summary_index).astype(jnp.float32)
    dattn_all = jnp.dot(out_grad, out_weight.T, preferred_element_type=jnp.float32).astype(jnp.bfloat16)
    causal = jnp.arange(STRIDE)[:, None] >= jnp.arange(STRIDE)[None, :]
    slot_block = jnp.arange(slots) // SUMMARY

    def step(carry, inputs):
        block, qs, ks, vs, das = inputs
        qf = qs.astype(jnp.float32)
        kf = ks.astype(jnp.float32)
        vf = vs.astype(jnp.float32)
        daf = das.astype(jnp.float32)
        visible = (slot_block < block)[None, None, :]
        s_loc = jnp.einsum('qhd,khd->hqk', qf, kf) * scale
        s_loc = jnp.where(causal[None], s_loc, -jnp.inf)
        s_sum = jnp.einsum('qhd,khd->hqk', qf, sum_keys) * scale
        s_sum = jnp.where(visible, s_sum, -jnp.inf)
        top = jnp.maximum(jnp.max(s_loc, axis=-1, keepdims=True), jnp.max(s_sum, axis=-1, keepdims=True))
        e_loc = jnp.exp(s_loc - top)
        e_sum = jnp.exp(s_sum - top)
        total = jnp.sum(e_loc, axis=-1, keepdims=True) + jnp.sum(e_sum, axis=-1, keepdims=True)
        p_loc = e_loc / total
        p_sum = e_sum / total
        pb_loc = p_loc.astype(jnp.bfloat16).astype(jnp.float32)
        pb_sum = p_sum.astype(jnp.bfloat16).astype(jnp.float32)
        attn = (jnp.einsum('hqk,khd->qhd', pb_loc, vf) + jnp.einsum('hqk,khd->qhd', pb_sum, sum_vals)).astype(jnp.bfloat16)
        dp_loc = jnp.einsum('qhd,khd->hqk', daf, vf)
        dp_sum = jnp.einsum('qhd,khd->hqk', daf, sum_vals)
        delta = jnp.sum(p_loc * dp_loc, axis=-1, keepdims=True) + jnp.sum(p_sum * dp_sum, axis=-1, keepdims=True)
        ds_loc = (p_loc * (dp_loc - delta)).astype(jnp.bfloat16).astype(jnp.float32)
        ds_sum = (p_sum * (dp_sum - delta)).astype(jnp.bfloat16).astype(jnp.float32)
        grad_q = (scale * (jnp.einsum('hqk,khd->qhd', ds_loc, kf) + jnp.einsum('hqk,khd->qhd', ds_sum, sum_keys))).astype(jnp.bfloat16)
        dk_loc = scale * jnp.einsum('hqk,qhd->khd', ds_loc, qf)
        dv_loc = jnp.einsum('hqk,qhd->khd', pb_loc, daf)
        new_k = carry[0] + scale * jnp.einsum('hqk,qhd->khd', ds_sum, qf)
        new_v = carry[1] + jnp.einsum('hqk,qhd->khd', pb_sum, daf)
        return (new_k, new_v), (attn, grad_q, dk_loc, dv_loc)

    shape4 = (STRIDES, STRIDE, HEADS, HEAD_DIM)
    xs = (jnp.arange(STRIDES).astype(jnp.int32), queries.reshape(shape4), key_rows.reshape(shape4),
          value_rows.reshape(shape4), dattn_all.reshape(shape4))
    zeros = jnp.zeros((slots, HEADS, HEAD_DIM), jnp.float32)
    (sum_dk, sum_dv), (attn, grad_q, dk_loc, dv_loc) = lax.scan(step, (zeros, zeros), xs)
    attn = attn.reshape(TOKENS, width)

    group_cols = width // N_HEAD
    attn_groups = attn.reshape(TOKENS, N_HEAD, group_cols).transpose(1, 0, 2)
    weight_groups = out_weight.reshape(N_HEAD, group_cols, D)

    def add_group(total, pieces):
        term = jnp.dot(pieces[0], pieces[1], preferred_element_type=jnp.float32)
        rounded = lax.optimization_barrier(term.astype(jnp.bfloat16)).astype(jnp.float32)
        return total + rounded, None

    projected, unused = lax.scan(add_group, jnp.zeros((TOKENS, D), jnp.float32), (attn_groups, weight_groups))
    attended = projected.astype(jnp.bfloat16)
    onehot = (jnp.arange(blocks)[None, :] == summary_index[:, None]).astype(jnp.float32)

    def spread(values):
        placed = onehot[:, :, None, None] * values.reshape(STRIDES, 1, SUMMARY, width)
        return placed.reshape(TOKENS, width)

    grad_key = (dk_loc.reshape(TOKENS, width) + spread(sum_dk)).astype(jnp.bfloat16)
    grad_value = (dv_loc.reshape(TOKENS, width) + spread(sum_dv)).astype(jnp.bfloat16)
    return attended, grad_q.reshape(TOKENS, width), grad_key, grad_value
```

```python
import functools

import jax
import jax.numpy as jnp
from jax import lax
from jax.experimental import pallas as pl
from jax.experimental.pallas import tpu as pltpu
from jax.sharding import PartitionSpec as P

HEAD_DIM = 128
SUMMARY = 8
SIZES = (8, 8, 8, 2)
MESH = pl.DeviceIdType.MESH
F32 = jnp.float32
BF16 = jnp.bfloat16
NT = (((1,), (1,)), ((), ()))
TN = (((0,), (0,)), ((), ()))
KA, KB, VA, VB, GK1, GK2, GV1, GV2 = range(8)


def dot(a, b, dims=(((1,), (0,)), ((), ()))):
    return lax.dot_general(a, b, dims, preferred_element_type=F32)


def kernel(sizes, idx_ref, q_ref, k_ref, v_ref, w_hbm, og_hbm,
           att_out, gq_out, gk_out, gv_out,
           w_v, og_v, tk, tv, sk, sv, da, attn, sloc, dploc, ploc, psum,
           ysend, yrecv, ysum, ring, kg, vg, rk, rv, s2k, s2v, r2k, r2v, dkl, dvl,
           load_sem, send_sem, recv_sem, psend_sem, precv_sem, rsend_sem, rrecv_sem):
    X, Z, Y, C = sizes
    N = Y * C
    rows, width = q_ref.shape
    heads = width // HEAD_DIM
    slots = X * Z * SUMMARY
    scale = HEAD_DIM ** (-0.5)
    ctx = lax.axis_index("ctx")
    head = lax.axis_index("head")
    mx, mz = ctx // Z, ctx % Z
    my, mc = head // C, head % C

    def at_x(d):
        return (((mx + d) % X) * Z + mz, head)

    def at_z(d):
        return (mx * Z + (mz + d) % Z, head)

    def at_y(d):
        return (ctx, ((my + Y + d) % Y) * C + mc)

    partner = (ctx, my * C + (1 - mc))

    def load_w(n):
        return pltpu.make_async_copy(w_hbm.at[:, pl.ds(n * width, width)], w_v.at[n], load_sem.at[0, n])

    def load_g(n):
        return pltpu.make_async_copy(og_hbm.at[:, pl.ds(n * width, width)], og_v.at[n], load_sem.at[1, n])

    for n in range(N):
        load_g(n).start()
        load_w(n).start()

    barrier = pltpu.get_barrier_semaphore()

    def greet(device):
        pl.semaphore_signal(barrier, inc=1, device_id=device, device_id_type=MESH)

    @pl.loop(1, X)
    def _(d):
        greet(at_x(d))

    @pl.loop(1, Z)
    def _(d):
        greet(at_z(d))

    greet(partner)
    greet(at_y(1))
    greet(at_y(-1))

    blocks = rows // SUMMARY
    index = idx_ref[0]
    chosen = lax.broadcasted_iota(jnp.int32, (blocks, SUMMARY, width), 0) == index

    def pick(ref):
        shaped = ref[...].astype(F32).reshape(blocks, SUMMARY, width)
        return jnp.sum(jnp.where(chosen, shaped, 0.0), axis=0).astype(BF16)

    tk[mx, mz] = pick(k_ref)
    tv[mx, mz] = pick(v_ref)
    pl.semaphore_wait(barrier, (X - 1) + (Z - 1) + 3)

    def copy(src, dst, phase, d, device):
        return pltpu.make_async_remote_copy(
            src_ref=src, dst_ref=dst, send_sem=send_sem.at[phase, d], recv_sem=recv_sem.at[phase, d],
            device_id=device, device_id_type=MESH)

    def ka(d):
        return copy(tk.at[mx, mz], tk.at[mx, mz], KA, d, at_z(d))

    def va(d):
        return copy(tv.at[mx, mz], tv.at[mx, mz], VA, d, at_x(d))

    def kb(d):
        return copy(tk.at[mx], tk.at[mx], KB, d, at_x(d))

    def vb(d):
        return copy(tv.at[:, mz], tv.at[:, mz], VB, d, at_z(d))

    def gk1(d):
        return copy(kg.at[(mx + d) % X], rk.at[mx], GK1, d, at_x(d))

    def gv1(d):
        return copy(vg.at[:, (mz + d) % Z], rv.at[mz], GV1, d, at_z(d))

    def gk2(d):
        return copy(s2k.at[(mz + d) % Z], r2k.at[mz], GK2, d, at_z(d))

    def gv2(d):
        return copy(s2v.at[(mx + d) % X], r2v.at[mx], GV2, d, at_x(d))

    def start(make, count):
        @pl.loop(1, count)
        def _(d):
            make(d).start()

    def arrive(make, count):
        @pl.loop(1, count)
        def _(d):
            make(d).wait_recv()

    def sent(make, count):
        @pl.loop(1, count)
        def _(d):
            make(d).wait_send()

    start(ka, Z)
    start(va, X)

    total = jnp.zeros((rows, width), F32)
    for n in range(N):
        load_g(n).wait()
        load_w(n).wait()
        total += dot(og_v[n], w_v[n], NT)
    da[...] = total.astype(BF16)

    arrive(ka, Z)
    start(kb, X)
    arrive(va, X)
    start(vb, Z)

    causal = (lax.broadcasted_iota(jnp.int32, (rows, rows), 0)
              >= lax.broadcasted_iota(jnp.int32, (rows, rows), 1))
    cols = [slice(h * HEAD_DIM, (h + 1) * HEAD_DIM) for h in range(heads)]
    for h in range(heads):
        sloc[h] = jnp.where(causal, dot(q_ref[:, cols[h]], k_ref[:, cols[h]], NT) * scale, -jnp.inf)
        dploc[h] = dot(da[:, cols[h]], v_ref[:, cols[h]], NT)

    arrive(kb, X)
    sk[...] = tk[...].astype(F32).reshape(slots, width).astype(BF16)
    arrive(vb, Z)
    sv[...] = tv[...].astype(F32).reshape(slots, width).astype(BF16)

    visible = lax.broadcasted_iota(jnp.int32, (rows, slots), 1) < ctx * SUMMARY
    for h in range(heads):
        s_loc = sloc[h]
        s_sum = jnp.where(visible, dot(q_ref[:, cols[h]], sk[:, cols[h]], NT) * scale, -jnp.inf)
        top = jnp.maximum(jnp.max(s_loc, axis=-1, keepdims=True), jnp.max(s_sum, axis=-1, keepdims=True))
        e_loc = jnp.exp(s_loc - top)
        e_sum = jnp.exp(s_sum - top)
        norm = jnp.sum(e_loc, axis=-1, keepdims=True) + jnp.sum(e_sum, axis=-1, keepdims=True)
        inverse = 1.0 / norm
        p_loc = e_loc * inverse
        p_sum = e_sum * inverse
        ploc[h] = p_loc
        psum[h] = p_sum
        attn[:, cols[h]] = (dot(p_loc.astype(BF16), v_ref[:, cols[h]])
                            + dot(p_sum.astype(BF16), sv[:, cols[h]])).astype(BF16)

    def pair(i):
        return pltpu.make_async_remote_copy(
            src_ref=ysend.at[i], dst_ref=yrecv.at[i], send_sem=psend_sem.at[i], recv_sem=precv_sem.at[i],
            device_id=partner, device_id_type=MESH)

    far = Y // 2

    def nth(i):
        return (my + far + i) % Y

    @pl.loop(0, Y)
    def _(i):
        to = nth(i)
        ysend[to] = dot(attn[...], w_v[to * C + (1 - mc)]).astype(BF16)
        pair(to).start()

    for h in range(heads):
        p_loc, p_sum = ploc[h], psum[h]
        da_h = da[:, cols[h]]
        q_h = q_ref[:, cols[h]]
        dp_loc = dploc[h]
        dp_sum = dot(da_h, sv[:, cols[h]], NT)
        delta = (jnp.sum(p_loc * dp_loc, axis=-1, keepdims=True)
                 + jnp.sum(p_sum * dp_sum, axis=-1, keepdims=True))
        ds_loc = (p_loc * (dp_loc - delta)).astype(BF16)
        ds_sum = (p_sum * (dp_sum - delta)).astype(BF16)
        kg[:, :, :, cols[h]] = (dot(ds_sum, q_h, TN) * scale).reshape(X, Z, SUMMARY, HEAD_DIM).astype(BF16)
        vg[:, :, :, cols[h]] = dot(p_sum.astype(BF16), da_h, TN).reshape(X, Z, SUMMARY, HEAD_DIM).astype(BF16)
        gq_out[:, cols[h]] = (scale * (dot(ds_loc, k_ref[:, cols[h]]) + dot(ds_sum, sk[:, cols[h]]))).astype(BF16)
        dkl[:, cols[h]] = scale * dot(ds_loc, q_h, TN)
        dvl[:, cols[h]] = dot(p_loc.astype(BF16), da_h, TN)

    start(gk1, X)
    start(gv1, Z)

    half = rows // 2
    chains = []
    for chunk in range(2):
        for way in (1, -1):
            hops = far if (chunk == 0) == (way == 1) else Y - 1 - far
            if hops:
                chains.append((chunk, way, hops))

    def hop(c, s):
        chunk, way, hops = chains[c]
        place = pl.ds(chunk * half, half)
        src = ysum.at[(my + Y + way * hops) % Y, place] if s == 0 else ring.at[c, s - 1]
        return pltpu.make_async_remote_copy(
            src_ref=src, dst_ref=ring.at[c, s], send_sem=rsend_sem.at[c, s], recv_sem=rrecv_sem.at[c, s],
            device_id=at_y(way), device_id_type=MESH)

    @pl.loop(0, Y)
    def _(i):
        to = nth(i)
        own = dot(attn[...], w_v[to * C + mc])
        pair(to).wait_recv()
        ysum[to] = (own + yrecv[to].astype(F32)).astype(BF16)

    for c in range(len(chains)):
        hop(c, 0).start()

    def relay(s):
        for c, (chunk, way, hops) in enumerate(chains):
            if s < hops:
                hop(c, s - 1).wait_recv()
                own = ysum[(my + Y + way * (hops - s)) % Y, chunk * half:(chunk + 1) * half]
                ring[c, s - 1] = (ring[c, s - 1].astype(F32) + own.astype(F32)).astype(BF16)
                hop(c, s).start()

    for s in range(1, far - 1):
        relay(s)

    arrive(gk1, X)

    def gathered(own, received, place, count):
        return lax.fori_loop(
            1, count, lambda d, acc: acc + received[(place + d) % count].astype(F32), own.astype(F32))

    s2k[...] = gathered(kg[mx], rk, mx, X).astype(BF16)
    start(gk2, Z)
    arrive(gv1, Z)
    s2v[...] = gathered(vg[:, mz], rv, mz, Z).astype(BF16)
    start(gv2, X)

    if far > 1:
        relay(far - 1)

    here = lax.broadcasted_iota(jnp.int32, (blocks, SUMMARY, width), 0) == index

    def spread(local, extra):
        shaped = local.reshape(blocks, SUMMARY, width)
        return jnp.where(here, shaped + extra[None], shaped).reshape(rows, width).astype(BF16)

    arrive(gk2, Z)
    gk_out[...] = spread(dkl[...], gathered(s2k[mz], r2k, mz, Z))
    arrive(gv2, X)
    gv_out[...] = spread(dvl[...], gathered(s2v[mx], r2v, mx, X))

    for chunk in range(2):
        place = slice(chunk * half, (chunk + 1) * half)
        value = ysum[my, place].astype(F32)
        for c, (which, way, hops) in enumerate(chains):
            if which == chunk:
                hop(c, hops - 1).wait_recv()
                value += ring[c, hops - 1].astype(F32)
        att_out[place, :] = value.astype(BF16)

    for make, count in ((ka, Z), (va, X), (kb, X), (vb, Z), (gk1, X), (gv1, Z), (gk2, Z), (gv2, X)):
        sent(make, count)

    @pl.loop(0, Y)
    def _(i):
        pair(i).wait_send()

    for c, (chunk, way, hops) in enumerate(chains):
        for s in range(hops):
            hop(c, s).wait_send()


def on_device(sizes, queries, key_rows, value_rows, summary_index, out_weight, out_grad):
    X, Z, Y, C = sizes
    rows, width = queries.shape
    heads = width // HEAD_DIM
    slots = X * Z * SUMMARY
    N = Y * C
    vmem = pl.BlockSpec(memory_space=pltpu.VMEM)
    hbm = pl.BlockSpec(memory_space=pl.ANY)
    out = jax.ShapeDtypeStruct((rows, width), BF16)
    table = (X, Z, SUMMARY, width)
    far = max(Y // 2, 1)
    scratch = [
        pltpu.VMEM((N, width, width), BF16),
        pltpu.VMEM((N, rows, width), BF16),
        pltpu.VMEM(table, BF16),
        pltpu.VMEM(table, BF16),
        pltpu.VMEM((slots, width), BF16),
        pltpu.VMEM((slots, width), BF16),
        pltpu.VMEM((rows, width), BF16),
        pltpu.VMEM((rows, width), BF16),
        pltpu.VMEM((heads, rows, rows), F32),
        pltpu.VMEM((heads, rows, rows), F32),
        pltpu.VMEM((heads, rows, rows), F32),
        pltpu.VMEM((heads, rows, slots), F32),
        pltpu.VMEM((Y, rows, width), BF16),
        pltpu.VMEM((Y, rows, width), BF16),
        pltpu.VMEM((Y, rows, width), BF16),
        pltpu.VMEM((4, far, rows // 2, width), BF16),
        pltpu.VMEM(table, BF16),
        pltpu.VMEM(table, BF16),
        pltpu.VMEM((X, Z, SUMMARY, width), BF16),
        pltpu.VMEM((Z, X, SUMMARY, width), BF16),
        pltpu.VMEM((Z, SUMMARY, width), BF16),
        pltpu.VMEM((X, SUMMARY, width), BF16),
        pltpu.VMEM((Z, SUMMARY, width), BF16),
        pltpu.VMEM((X, SUMMARY, width), BF16),
        pltpu.VMEM((rows, width), F32),
        pltpu.VMEM((rows, width), F32),
        pltpu.SemaphoreType.DMA((2, N)),
        pltpu.SemaphoreType.DMA((8, max(X, Z))),
        pltpu.SemaphoreType.DMA((8, max(X, Z))),
        pltpu.SemaphoreType.DMA((Y,)),
        pltpu.SemaphoreType.DMA((Y,)),
        pltpu.SemaphoreType.DMA((4, far)),
        pltpu.SemaphoreType.DMA((4, far)),
    ]
    return tuple(pl.pallas_call(
        functools.partial(kernel, sizes),
        out_shape=(out, out, out, out),
        in_specs=[pl.BlockSpec(memory_space=pltpu.SMEM), vmem, vmem, vmem, hbm, hbm],
        out_specs=(vmem, vmem, vmem, vmem),
        scratch_shapes=scratch,
        compiler_params=pltpu.CompilerParams(collective_id=0, has_side_effects=True),
        name="sparse_attention_step",
    )(summary_index, queries, key_rows, value_rows, out_weight, out_grad))


def solution(mesh, sizes=SIZES):
    return jax.shard_map(
        functools.partial(on_device, sizes),
        mesh=mesh,
        in_specs=(
            P("ctx", "head"),
            P("ctx", "head"),
            P("ctx", "head"),
            P("ctx"),
            P("head", None),
            P("ctx", None),
        ),
        out_specs=(P("ctx", "head"), P("ctx", "head"), P("ctx", "head"), P("ctx", "head")),
        check_vma=False,
    )
```

```python
import functools

import jax
import jax.numpy as jnp
from jax import lax
from jax.experimental import pallas as pl
from jax.experimental.pallas import tpu as pltpu
from jax.sharding import PartitionSpec as P

HEAD_DIM = 128
SUMMARY = 8
CHUNKS = 4
SIZES = (8, 8, 8, 2)
MESH = pl.DeviceIdType.MESH
F32 = jnp.float32
BF16 = jnp.bfloat16
NT = (((1,), (1,)), ((), ()))
TN = (((0,), (0,)), ((), ()))
KA, VA, GK2, GV2 = range(4)


def dot(a, b, dims=(((1,), (0,)), ((), ()))):
    return lax.dot_general(a, b, dims, preferred_element_type=F32)


def kernel(sizes, idx_hbm, q_hbm, k_hbm, v_hbm, w_hbm, og_hbm,
           att_out, gq_out, gk_out, gv_out,
           idx_ref, q_ref, k_ref, v_ref, w_v, og_v, tk, tv, sk, da, attn, sloc, dploc, dsloc, pbloc, dssum,
           w_p, ysum, ring, kg, vg, rk, rv, s2k, s2v, r2k, r2v, dkl, dvl,
           load_sem, in_sem, send_sem, recv_sem, psend_sem, precv_sem, rsend_sem, rrecv_sem):
    X, Z, Y, C = sizes
    N = Y * C
    rows, width = q_ref.shape
    heads = width // HEAD_DIM
    slots = X * Z * SUMMARY
    scale = HEAD_DIM ** (-0.5)
    ctx = lax.axis_index("ctx")
    head = lax.axis_index("head")
    mx, mz = ctx // Z, ctx % Z
    my, mc = head // C, head % C

    def at_x(d):
        return (((mx + d) % X) * Z + mz, head)

    def at_z(d):
        return (mx * Z + (mz + d) % Z, head)

    def at_y(d):
        return (ctx, ((my + Y + d) % Y) * C + mc)

    partner = (ctx, my * C + (1 - mc))

    def load_w(n):
        return pltpu.make_async_copy(w_hbm.at[:, pl.ds(n * width, width)], w_v.at[n], load_sem.at[0, n])

    def load_g(n):
        return pltpu.make_async_copy(og_hbm.at[:, pl.ds(n * width, width)], og_v.at[n], load_sem.at[1, n])

    barrier = pltpu.get_barrier_semaphore()

    def greet(device):
        pl.semaphore_signal(barrier, inc=1, device_id=device, device_id_type=MESH)

    @pl.loop(1, X)
    def _(d):
        greet(at_x(d))

    @pl.loop(1, Z)
    def _(d):
        greet(at_z(d))

    greet(partner)
    greet(at_y(1))
    greet(at_y(-1))

    loads = [pltpu.make_async_copy(a, b, in_sem.at[i]) for i, (a, b) in enumerate(
        ((idx_hbm, idx_ref), (k_hbm, k_ref), (v_hbm, v_ref), (q_hbm, q_ref)))]
    for load in loads:
        load.start()

    @pl.loop(0, N)
    def _(n):
        load_g(n).start()
        load_w(n).start()

    for load in loads:
        load.wait()

    blocks = rows // SUMMARY
    index = idx_ref[0]
    cols = [slice(h * HEAD_DIM, (h + 1) * HEAD_DIM) for h in range(heads)]
    chosen = lax.broadcasted_iota(jnp.int32, (blocks, SUMMARY, HEAD_DIM), 0) == index

    def pick(ref, h):
        shaped = ref[:, cols[h]].astype(F32).reshape(blocks, SUMMARY, HEAD_DIM)
        return jnp.sum(jnp.where(chosen, shaped, 0.0), axis=0).astype(BF16)

    for h in range(heads):
        tk[h, mx, mz] = pick(k_ref, h)
        tv[h, mz, mx] = pick(v_ref, h)
    pl.semaphore_wait(barrier, (X - 1) + (Z - 1) + 3)

    def copy(src, dst, phase, d, device):
        return pltpu.make_async_remote_copy(
            src_ref=src, dst_ref=dst, send_sem=send_sem.at[phase, d], recv_sem=recv_sem.at[phase, d],
            device_id=device, device_id_type=MESH)

    KB1, VB1, GK1, GV1 = (4 + i * heads for i in range(4))

    def ka(d):
        return copy(tk.at[:, mx, mz], tk.at[:, mx, mz], KA, d, at_z(d))

    def va(d):
        return copy(tv.at[:, mz, mx], tv.at[:, mz, mx], VA, d, at_x(d))

    def kb(h):
        return lambda d: copy(tk.at[h, mx], tk.at[h, mx], KB1 + h, d, at_x(d))

    def vb(h):
        return lambda d: copy(tv.at[h, mz], tv.at[h, mz], VB1 + h, d, at_z(d))

    def gk1(h):
        return lambda d: copy(kg.at[h, (mx + d) % X], rk.at[h, mx], GK1 + h, d, at_x(d))

    def gv1(h):
        return lambda d: copy(vg.at[h, (mz + d) % Z], rv.at[h, mz], GV1 + h, d, at_z(d))

    def gk2(d):
        return copy(s2k.at[:, (mz + d) % Z], r2k.at[mz], GK2, d, at_z(d))

    def gv2(d):
        return copy(s2v.at[:, (mx + d) % X], r2v.at[mx], GV2, d, at_x(d))

    def start(make, count):
        @pl.loop(1, count)
        def _(d):
            make(d).start()

    def arrive(make, count):
        @pl.loop(1, count)
        def _(d):
            make(d).wait_recv()

    def sent(make, count):
        @pl.loop(1, count)
        def _(d):
            make(d).wait_send()

    def lend(i):
        return pltpu.make_async_remote_copy(
            src_ref=w_hbm.at[:, pl.ds((i * C + (1 - mc)) * width, width)], dst_ref=w_p.at[i],
            send_sem=psend_sem.at[i], recv_sem=precv_sem.at[i], device_id=partner, device_id_type=MESH)

    def share(h):
        return pltpu.make_async_remote_copy(
            src_ref=attn.at[:, pl.ds(h * HEAD_DIM, HEAD_DIM)],
            dst_ref=attn.at[:, pl.ds(width + h * HEAD_DIM, HEAD_DIM)],
            send_sem=psend_sem.at[Y + h], recv_sem=precv_sem.at[Y + h], device_id=partner, device_id_type=MESH)

    start(ka, Z)
    start(va, X)

    @pl.loop(0, Y)
    def _(i):
        lend(i).start()

    total = jnp.zeros((rows, width), F32)
    for n in range(N):
        load_g(n).wait()
        load_w(n).wait()
        total += dot(og_v[n], w_v[n], NT)
    da[...] = total.astype(BF16)

    arrive(ka, Z)
    start(kb(0), X)
    arrive(va, X)
    start(vb(0), Z)
    for h in range(1, heads):
        start(kb(h), X)
        start(vb(h), Z)

    causal = (lax.broadcasted_iota(jnp.int32, (rows, rows), 0)
              >= lax.broadcasted_iota(jnp.int32, (rows, rows), 1))
    for h in range(heads):
        sloc[h] = jnp.where(causal, dot(q_ref[:, cols[h]], k_ref[:, cols[h]], NT) * scale, -jnp.inf)
        dploc[h] = dot(da[:, cols[h]], v_ref[:, cols[h]], NT)

    visible = lax.broadcasted_iota(jnp.int32, (rows, slots), 1) < ctx * SUMMARY
    for h in range(heads):
        q_h, v_h, da_h = q_ref[:, cols[h]], v_ref[:, cols[h]], da[:, cols[h]]
        arrive(kb(h), X)
        sk[h] = tk[h].astype(F32).reshape(slots, HEAD_DIM).astype(BF16)
        s_loc = sloc[h]
        s_sum = jnp.where(visible, dot(q_h, sk[h], NT) * scale, -jnp.inf)
        top = jnp.maximum(jnp.max(s_loc, axis=-1, keepdims=True), jnp.max(s_sum, axis=-1, keepdims=True))
        e_loc = jnp.exp(s_loc - top)
        e_sum = jnp.exp(s_sum - top)
        norm = jnp.sum(e_loc, axis=-1, keepdims=True) + jnp.sum(e_sum, axis=-1, keepdims=True)
        inverse = 1.0 / norm
        p_loc = e_loc * inverse
        p_sum = e_sum * inverse
        arrive(vb(h), Z)
        sv_h = jnp.swapaxes(tv[h].astype(F32), 0, 1).reshape(slots, HEAD_DIM).astype(BF16)
        pb_loc, pb_sum = p_loc.astype(BF16), p_sum.astype(BF16)
        attn[:, cols[h]] = (dot(pb_loc, v_h) + dot(pb_sum, sv_h)).astype(BF16)
        share(h).start()
        dp_loc = dploc[h]
        dp_sum = dot(da_h, sv_h, NT)
        delta = (jnp.sum(p_loc * dp_loc, axis=-1, keepdims=True)
                 + jnp.sum(p_sum * dp_sum, axis=-1, keepdims=True))
        ds_sum = (p_sum * (dp_sum - delta)).astype(BF16)
        kg[h] = (dot(ds_sum, q_h, TN) * scale).reshape(X, Z, SUMMARY, HEAD_DIM).astype(BF16)
        vg[h] = jnp.swapaxes(dot(pb_sum, da_h, TN).reshape(X, Z, SUMMARY, HEAD_DIM), 0, 1).astype(BF16)
        start(gk1(h), X)
        start(gv1(h), Z)
        dsloc[h] = (p_loc * (dp_loc - delta)).astype(BF16)
        dssum[h] = ds_sum
        pbloc[h] = pb_loc

    far = Y // 2

    order = sorted(range(Y), key=lambda i: -min(i, Y - i))

    @pl.loop(0, Y)
    def _(i):
        lend(i).wait_recv()

    for h in range(heads):
        share(h).wait_recv()

    part = rows // CHUNKS
    chains = []
    for chunk in range(CHUNKS):
        for way in (1, -1):
            hops = far if (chunk % 2 == 0) == (way == 1) else Y - 1 - far
            if hops:
                chains.append((chunk, way, hops))

    def hop(c, s):
        chunk, way, hops = chains[c]
        place = pl.ds(chunk * part, part)
        src = ysum.at[(my + Y + way * hops) % Y, place] if s == 0 else ring.at[c, s - 1]
        return pltpu.make_async_remote_copy(
            src_ref=src, dst_ref=ring.at[c, s], send_sem=rsend_sem.at[c, s], recv_sem=rrecv_sem.at[c, s],
            device_id=at_y(way), device_id_type=MESH)

    def combine(i):
        to = (my + i) % Y
        own = dot(attn[:, :width], w_v[to * C + mc])
        ysum[to] = (own + dot(attn[:, width:], w_p[to])).astype(BF16)

    begun = set()
    for n, i in enumerate(order):
        combine(i)
        for c, (chunk, way, hops) in enumerate(chains):
            if c not in begun and (way * hops) % Y in order[:n + 1]:
                begun.add(c)
                hop(c, 0).start()

    def relay(s):
        for c, (chunk, way, hops) in enumerate(chains):
            if s < hops:
                hop(c, s - 1).wait_recv()
                own = ysum[(my + Y + way * (hops - s)) % Y, chunk * part:(chunk + 1) * part]
                ring[c, s - 1] = (ring[c, s - 1].astype(F32) + own.astype(F32)).astype(BF16)
                hop(c, s).start()

    def gathered(own, received, place, count):
        total = own.astype(F32)
        for d in range(1, count):
            total += received[(place + d) % count].astype(F32)
        return total

    def local_grads(h):
        q_h, da_h = q_ref[:, cols[h]], da[:, cols[h]]
        gq_out[:, cols[h]] = (scale * (dot(dsloc[h], k_ref[:, cols[h]]) + dot(dssum[h], sk[h]))).astype(BF16)
        dkl[h] = scale * dot(dsloc[h], q_h, TN)
        dvl[h] = dot(pbloc[h], da_h, TN)

    for h in range(heads):
        local_grads(h)

    for s in range(1, far - 1):
        relay(s)

    for h in range(heads):
        arrive(gk1(h), X)
        s2k[h] = gathered(kg[h, mx], rk.at[h], mx, X).astype(BF16)
    start(gk2, Z)
    for h in range(heads):
        arrive(gv1(h), Z)
        s2v[h] = gathered(vg[h, mz], rv.at[h], mz, Z).astype(BF16)
    start(gv2, X)

    if far > 1:
        relay(far - 1)

    for chunk in range(CHUNKS):
        place = slice(chunk * part, (chunk + 1) * part)
        value = ysum[my, place].astype(F32)
        for c, (which, way, hops) in enumerate(chains):
            if which == chunk:
                hop(c, hops - 1).wait_recv()
                value += ring[c, hops - 1].astype(F32)
        att_out[place, :] = value.astype(BF16)

    def spread(local, extra):
        shaped = local.reshape(blocks, SUMMARY, HEAD_DIM)
        return jnp.where(chosen, shaped + extra[None], shaped).reshape(rows, HEAD_DIM).astype(BF16)

    arrive(gk2, Z)
    sum_dk = gathered(s2k[:, mz], r2k, mz, Z)
    for h in range(heads):
        gk_out[:, cols[h]] = spread(dkl[h], sum_dk[h])
    arrive(gv2, X)
    sum_dv = gathered(s2v[:, mx], r2v, mx, X)
    for h in range(heads):
        gv_out[:, cols[h]] = spread(dvl[h], sum_dv[h])

    for make, count in ((ka, Z), (va, X), (gk2, Z), (gv2, X)):
        sent(make, count)
    for h in range(heads):
        for make, count in ((kb, X), (vb, Z), (gk1, X), (gv1, Z)):
            sent(make(h), count)

    @pl.loop(0, Y)
    def _(i):
        lend(i).wait_send()

    for h in range(heads):
        share(h).wait_send()

    for c, (chunk, way, hops) in enumerate(chains):
        for s in range(hops):
            hop(c, s).wait_send()


def store(*refs):
    sources, targets, sem = refs[:4], refs[4:8], refs[8]
    copies = [pltpu.make_async_copy(a, b, sem.at[i]) for i, (a, b) in enumerate(zip(sources, targets))]
    for c in copies:
        c.start()
    for c in copies:
        c.wait()


def on_device(sizes, queries, key_rows, value_rows, summary_index, out_weight, out_grad):
    X, Z, Y, C = sizes
    rows, width = queries.shape
    heads = width // HEAD_DIM
    slots = X * Z * SUMMARY
    N = Y * C
    vmem = pl.BlockSpec(memory_space=pltpu.VMEM)
    hbm = pl.BlockSpec(memory_space=pl.ANY)
    out = jax.ShapeDtypeStruct((rows, width), BF16)
    table = (heads, X, Z, SUMMARY, HEAD_DIM)
    across = (heads, Z, X, SUMMARY, HEAD_DIM)
    far = max(Y // 2, 1)
    scratch = [
        pltpu.SMEM((1,), jnp.int32),
        pltpu.VMEM((rows, width), BF16),
        pltpu.VMEM((rows, width), BF16),
        pltpu.VMEM((rows, width), BF16),
        pltpu.VMEM((N, width, width), BF16),
        pltpu.VMEM((N, rows, width), BF16),
        pltpu.VMEM(table, BF16),
        pltpu.VMEM(across, BF16),
        pltpu.VMEM((heads, slots, HEAD_DIM), BF16),
        pltpu.VMEM((rows, width), BF16),
        pltpu.VMEM((rows, 2 * width), BF16),
        pltpu.VMEM((heads, rows, rows), F32),
        pltpu.VMEM((heads, rows, rows), F32),
        pltpu.VMEM((heads, rows, rows), BF16),
        pltpu.VMEM((heads, rows, rows), BF16),
        pltpu.VMEM((heads, rows, slots), BF16),
        pltpu.VMEM((Y, width, width), BF16),
        pltpu.VMEM((Y, rows, width), BF16),
        pltpu.VMEM((2 * CHUNKS, far, rows // CHUNKS, width), BF16),
        pltpu.VMEM(table, BF16),
        pltpu.VMEM(across, BF16),
        pltpu.VMEM((heads, X, Z, SUMMARY, HEAD_DIM), BF16),
        pltpu.VMEM((heads, Z, X, SUMMARY, HEAD_DIM), BF16),
        pltpu.VMEM((heads, Z, SUMMARY, HEAD_DIM), BF16),
        pltpu.VMEM((heads, X, SUMMARY, HEAD_DIM), BF16),
        pltpu.VMEM((Z, heads, SUMMARY, HEAD_DIM), BF16),
        pltpu.VMEM((X, heads, SUMMARY, HEAD_DIM), BF16),
        pltpu.VMEM((heads, rows, HEAD_DIM), F32),
        pltpu.VMEM((heads, rows, HEAD_DIM), F32),
        pltpu.SemaphoreType.DMA((2, N)),
        pltpu.SemaphoreType.DMA((4,)),
        pltpu.SemaphoreType.DMA((4 + 4 * heads, max(X, Z))),
        pltpu.SemaphoreType.DMA((4 + 4 * heads, max(X, Z))),
        pltpu.SemaphoreType.DMA((Y + heads,)),
        pltpu.SemaphoreType.DMA((Y + heads,)),
        pltpu.SemaphoreType.DMA((2 * CHUNKS, far)),
        pltpu.SemaphoreType.DMA((2 * CHUNKS, far)),
    ]
    held = pltpu.VMEM((rows, width), BF16)
    results = pl.pallas_call(
        functools.partial(kernel, sizes),
        out_shape=(held, held, held, held),
        in_specs=[hbm] * 6,
        out_specs=(vmem, vmem, vmem, vmem),
        scratch_shapes=scratch,
        compiler_params=pltpu.CompilerParams(collective_id=0, has_side_effects=True),
        name="sparse_attention_step",
    )(summary_index, queries, key_rows, value_rows, out_weight, out_grad)
    return tuple(pl.pallas_call(
        store,
        out_shape=(out, out, out, out),
        in_specs=[vmem] * 4,
        out_specs=(hbm,) * 4,
        scratch_shapes=[pltpu.SemaphoreType.DMA((4,))],
        name="store_results",
    )(*[pltpu.with_memory_space_constraint(r, pltpu.VMEM) for r in results]))


def solution(mesh, sizes=SIZES):
    return jax.shard_map(
        functools.partial(on_device, sizes),
        mesh=mesh,
        in_specs=(
            P("ctx", "head"),
            P("ctx", "head"),
            P("ctx", "head"),
            P("ctx"),
            P("head", None),
            P("ctx", None),
        ),
        out_specs=(P("ctx", "head"), P("ctx", "head"), P("ctx", "head"), P("ctx", "head")),
        check_vma=False,
    )
```

```python
import functools

import jax
import jax.numpy as jnp
from jax import lax
from jax.experimental import pallas as pl
from jax.experimental.pallas import tpu as pltpu
from jax.sharding import PartitionSpec as P

HEAD_DIM = 128
SUMMARY = 8
CHUNKS = 4
SIZES = (8, 8, 8, 2)
MESH = pl.DeviceIdType.MESH
F32 = jnp.float32
BF16 = jnp.bfloat16
NT = (((1,), (1,)), ((), ()))
TN = (((0,), (0,)), ((), ()))
KA, VA, GK2, GV2 = range(4)


def dot(a, b, dims=(((1,), (0,)), ((), ()))):
    return lax.dot_general(a, b, dims, preferred_element_type=F32)


def kernel(sizes, idx_hbm, q_hbm, k_hbm, v_hbm, w_hbm, og_hbm,
           att_out, gq_out, gk_out, gv_out,
           idx_ref, q_ref, k_ref, v_ref, w_v, og_v, sums, tk, tv, sk, da, attn, sloc, dploc, dsloc, pbloc, dssum,
           w_p, ysum, ring, kg, vg, rk, rv, s2k, s2v, r2k, r2v, dkl, dvl,
           load_sem, in_sem, send_sem, recv_sem, psend_sem, precv_sem, rsend_sem, rrecv_sem):
    X, Z, Y, C = sizes
    N = Y * C
    rows, width = q_ref.shape
    heads = width // HEAD_DIM
    slots = X * Z * SUMMARY
    scale = HEAD_DIM ** (-0.5)
    ctx = lax.axis_index("ctx")
    head = lax.axis_index("head")
    mx, mz = ctx // Z, ctx % Z
    my, mc = head // C, head % C

    def at_x(d):
        return (((mx + d) % X) * Z + mz, head)

    def at_z(d):
        return (mx * Z + (mz + d) % Z, head)

    def at_y(d):
        return (ctx, ((my + Y + d) % Y) * C + mc)

    partner = (ctx, my * C + (1 - mc))

    def load_w(n):
        return pltpu.make_async_copy(w_hbm.at[:, pl.ds(n * width, width)], w_v.at[n], load_sem.at[0, n])

    def load_g(n):
        return pltpu.make_async_copy(og_hbm.at[:, pl.ds(n * width, width)], og_v.at[n], load_sem.at[1, n])

    barrier = pltpu.get_barrier_semaphore()

    def greet(device):
        pl.semaphore_signal(barrier, inc=1, device_id=device, device_id_type=MESH)

    @pl.loop(1, X)
    def _(d):
        greet(at_x(d))

    @pl.loop(1, Z)
    def _(d):
        greet(at_z(d))

    greet(partner)
    greet(at_y(1))
    greet(at_y(-1))

    loads = [pltpu.make_async_copy(a, b, in_sem.at[i]) for i, (a, b) in enumerate(
        ((idx_hbm, idx_ref), (k_hbm, k_ref), (v_hbm, v_ref), (q_hbm, q_ref)))]
    for load in loads:
        load.start()

    @pl.loop(0, N)
    def _(n):
        load_g(n).start()
        load_w(n).start()

    for load in loads:
        load.wait()

    blocks = rows // SUMMARY
    index = idx_ref[0]
    cols = [slice(h * HEAD_DIM, (h + 1) * HEAD_DIM) for h in range(heads)]
    chosen = lax.broadcasted_iota(jnp.int32, (blocks, SUMMARY, HEAD_DIM), 0) == index

    def pick(ref, h):
        shaped = ref[:, cols[h]].astype(F32).reshape(blocks, SUMMARY, HEAD_DIM)
        return jnp.sum(jnp.where(chosen, shaped, 0.0), axis=0).astype(BF16)

    for h in range(heads):
        tk[h, mx, mz] = pick(k_ref, h)
        tv[h, mz, mx] = pick(v_ref, h)
    pl.semaphore_wait(barrier, (X - 1) + (Z - 1) + 3)

    def copy(src, dst, phase, d, device):
        return pltpu.make_async_remote_copy(
            src_ref=src, dst_ref=dst, send_sem=send_sem.at[phase, d], recv_sem=recv_sem.at[phase, d],
            device_id=device, device_id_type=MESH)

    KB1, VB1, GK1, GV1 = (4 + i * heads for i in range(4))

    def ka(d):
        return copy(tk.at[:, mx, mz], tk.at[:, mx, mz], KA, d, at_z(d))

    def va(d):
        return copy(tv.at[:, mz, mx], tv.at[:, mz, mx], VA, d, at_x(d))

    def kb(h):
        return lambda d: copy(tk.at[h, mx], tk.at[h, mx], KB1 + h, d, at_x(d))

    def vb(h):
        return lambda d: copy(tv.at[h, mz], tv.at[h, mz], VB1 + h, d, at_z(d))

    def gk1(h):
        return lambda d: copy(kg.at[h, (mx + d) % X], rk.at[h, mx], GK1 + h, d, at_x(d))

    def gv1(h):
        return lambda d: copy(vg.at[h, (mz + d) % Z], rv.at[h, mz], GV1 + h, d, at_z(d))

    def gk2(d):
        return copy(s2k.at[:, (mz + d) % Z], r2k.at[mz], GK2, d, at_z(d))

    def gv2(d):
        return copy(s2v.at[:, (mx + d) % X], r2v.at[mx], GV2, d, at_x(d))

    def start(make, count):
        @pl.loop(0, count - 1)
        def _(i):
            make(count // 2 + ((i + 1) // 2) * (2 * (i % 2) - 1)).start()

    def arrive(make, count):
        @pl.loop(1, count)
        def _(d):
            make(d).wait_recv()

    def sent(make, count):
        @pl.loop(1, count)
        def _(d):
            make(d).wait_send()

    def lend(i):
        return pltpu.make_async_remote_copy(
            src_ref=w_hbm.at[:, pl.ds((i * C + (1 - mc)) * width, width)], dst_ref=w_p.at[i],
            send_sem=psend_sem.at[i], recv_sem=precv_sem.at[i], device_id=partner, device_id_type=MESH)

    def share(h):
        return pltpu.make_async_remote_copy(
            src_ref=attn.at[:, pl.ds(h * HEAD_DIM, HEAD_DIM)],
            dst_ref=attn.at[:, pl.ds(width + h * HEAD_DIM, HEAD_DIM)],
            send_sem=psend_sem.at[Y + h], recv_sem=precv_sem.at[Y + h], device_id=partner, device_id_type=MESH)

    start(ka, Z)
    start(va, X)

    @pl.loop(0, Y)
    def _(i):
        lend(i).start()

    arrive(ka, Z)
    start(kb(0), X)
    arrive(va, X)
    start(vb(0), Z)
    for h in range(1, heads):
        if h == heads - 1:
            sums[...] = jnp.zeros((rows, width), F32)

            @pl.loop(0, N)
            def _(n):
                load_g(n).wait()
                load_w(n).wait()
                sums[...] += dot(og_v[n], w_v[n], NT)

            da[...] = sums[...].astype(BF16)

        start(kb(h), X)
        start(vb(h), Z)

    causal = (lax.broadcasted_iota(jnp.int32, (rows, rows), 0)
              >= lax.broadcasted_iota(jnp.int32, (rows, rows), 1))
    for h in range(heads):
        sloc[h] = jnp.where(causal, dot(q_ref[:, cols[h]], k_ref[:, cols[h]], NT) * scale, -jnp.inf)
        dploc[h] = dot(da[:, cols[h]], v_ref[:, cols[h]], NT)

    visible = lax.broadcasted_iota(jnp.int32, (rows, slots), 1) < ctx * SUMMARY
    for h in range(heads):
        q_h, v_h, da_h = q_ref[:, cols[h]], v_ref[:, cols[h]], da[:, cols[h]]
        arrive(kb(h), X)
        sk[h] = tk[h].astype(F32).reshape(slots, HEAD_DIM).astype(BF16)
        s_loc = sloc[h]
        s_sum = jnp.where(visible, dot(q_h, sk[h], NT) * scale, -jnp.inf)
        top = jnp.maximum(jnp.max(s_loc, axis=-1, keepdims=True), jnp.max(s_sum, axis=-1, keepdims=True))
        e_loc = jnp.exp(s_loc - top)
        e_sum = jnp.exp(s_sum - top)
        norm = jnp.sum(e_loc, axis=-1, keepdims=True) + jnp.sum(e_sum, axis=-1, keepdims=True)
        inverse = 1.0 / norm
        p_loc = e_loc * inverse
        p_sum = e_sum * inverse
        arrive(vb(h), Z)
        sv_h = jnp.swapaxes(tv[h].astype(F32), 0, 1).reshape(slots, HEAD_DIM).astype(BF16)
        pb_loc, pb_sum = p_loc.astype(BF16), p_sum.astype(BF16)
        attn[:, cols[h]] = (dot(pb_loc, v_h) + dot(pb_sum, sv_h)).astype(BF16)
        share(h).start()
        dp_loc = dploc[h]
        dp_sum = dot(da_h, sv_h, NT)
        delta = (jnp.sum(p_loc * dp_loc, axis=-1, keepdims=True)
                 + jnp.sum(p_sum * dp_sum, axis=-1, keepdims=True))
        ds_sum = (p_sum * (dp_sum - delta)).astype(BF16)
        kg[h] = (dot(ds_sum, q_h, TN) * scale).reshape(X, Z, SUMMARY, HEAD_DIM).astype(BF16)
        vg[h] = jnp.swapaxes(dot(pb_sum, da_h, TN).reshape(X, Z, SUMMARY, HEAD_DIM), 0, 1).astype(BF16)
        start(gk1(h), X)
        start(gv1(h), Z)
        dsloc[h] = (p_loc * (dp_loc - delta)).astype(BF16)
        dssum[h] = ds_sum
        pbloc[h] = pb_loc

    far = Y // 2

    order = sorted(range(Y), key=lambda i: -min(i, Y - i))

    @pl.loop(0, Y)
    def _(i):
        lend(i).wait_recv()

    for h in range(heads):
        share(h).wait_recv()

    part = rows // CHUNKS
    chains = []
    for chunk in range(CHUNKS):
        for way in (1, -1):
            hops = far if (chunk % 2 == 0) == (way == 1) else Y - 1 - far
            if hops:
                chains.append((chunk, way, hops))

    def hop(c, s):
        chunk, way, hops = chains[c]
        place = pl.ds(chunk * part, part)
        src = ysum.at[(my + Y + way * hops) % Y, place] if s == 0 else ring.at[c, s - 1]
        return pltpu.make_async_remote_copy(
            src_ref=src, dst_ref=ring.at[c, s], send_sem=rsend_sem.at[c, s], recv_sem=rrecv_sem.at[c, s],
            device_id=at_y(way), device_id_type=MESH)

    def combine(i):
        to = (my + i) % Y
        own = dot(attn[:, :width], w_v[to * C + mc])
        ysum[to] = (own + dot(attn[:, width:], w_p[to])).astype(BF16)

    begun = set()
    for n, i in enumerate(order):
        combine(i)
        for c, (chunk, way, hops) in enumerate(chains):
            if c not in begun and (way * hops) % Y in order[:n + 1]:
                begun.add(c)
                hop(c, 0).start()

    def relay(s):
        for c, (chunk, way, hops) in enumerate(chains):
            if s < hops:
                hop(c, s - 1).wait_recv()
                own = ysum[(my + Y + way * (hops - s)) % Y, chunk * part:(chunk + 1) * part]
                ring[c, s - 1] = (ring[c, s - 1].astype(F32) + own.astype(F32)).astype(BF16)
                hop(c, s).start()

    def gathered(own, received, place, count):
        total = own.astype(F32)
        for d in range(1, count):
            total += received[(place + d) % count].astype(F32)
        return total

    def local_grads(h):
        q_h, da_h = q_ref[:, cols[h]], da[:, cols[h]]
        gq_out[:, cols[h]] = (scale * (dot(dsloc[h], k_ref[:, cols[h]]) + dot(dssum[h], sk[h]))).astype(BF16)
        dkl[h] = scale * dot(dsloc[h], q_h, TN)
        dvl[h] = dot(pbloc[h], da_h, TN)

    for h in range(heads):
        local_grads(h)

    for s in range(1, far - 1):
        relay(s)

    for h in range(heads):
        arrive(gk1(h), X)
        s2k[h] = gathered(kg[h, mx], rk.at[h], mx, X).astype(BF16)
    start(gk2, Z)
    for h in range(heads):
        arrive(gv1(h), Z)
        s2v[h] = gathered(vg[h, mz], rv.at[h], mz, Z).astype(BF16)
    start(gv2, X)

    if far > 1:
        relay(far - 1)

    for chunk in range(CHUNKS):
        place = slice(chunk * part, (chunk + 1) * part)
        value = ysum[my, place].astype(F32)
        for c, (which, way, hops) in enumerate(chains):
            if which == chunk:
                hop(c, hops - 1).wait_recv()
                value += ring[c, hops - 1].astype(F32)
        att_out[place, :] = value.astype(BF16)

    def spread(local, extra):
        shaped = local.reshape(blocks, SUMMARY, HEAD_DIM)
        return jnp.where(chosen, shaped + extra[None], shaped).reshape(rows, HEAD_DIM).astype(BF16)

    arrive(gk2, Z)
    sum_dk = gathered(s2k[:, mz], r2k, mz, Z)
    for h in range(heads):
        gk_out[:, cols[h]] = spread(dkl[h], sum_dk[h])
    arrive(gv2, X)
    sum_dv = gathered(s2v[:, mx], r2v, mx, X)
    for h in range(heads):
        gv_out[:, cols[h]] = spread(dvl[h], sum_dv[h])

    for make, count in ((ka, Z), (va, X), (gk2, Z), (gv2, X)):
        sent(make, count)
    for h in range(heads):
        for make, count in ((kb, X), (vb, Z), (gk1, X), (gv1, Z)):
            sent(make(h), count)

    @pl.loop(0, Y)
    def _(i):
        lend(i).wait_send()

    for h in range(heads):
        share(h).wait_send()

    for c, (chunk, way, hops) in enumerate(chains):
        for s in range(hops):
            hop(c, s).wait_send()


def store(*refs):
    sources, targets, sem = refs[:4], refs[4:8], refs[8]
    copies = [pltpu.make_async_copy(a, b, sem.at[i]) for i, (a, b) in enumerate(zip(sources, targets))]
    for c in copies:
        c.start()
    for c in copies:
        c.wait()


def on_device(sizes, queries, key_rows, value_rows, summary_index, out_weight, out_grad):
    X, Z, Y, C = sizes
    rows, width = queries.shape
    heads = width // HEAD_DIM
    slots = X * Z * SUMMARY
    N = Y * C
    vmem = pl.BlockSpec(memory_space=pltpu.VMEM)
    hbm = pl.BlockSpec(memory_space=pl.ANY)
    out = jax.ShapeDtypeStruct((rows, width), BF16)
    table = (heads, X, Z, SUMMARY, HEAD_DIM)
    across = (heads, Z, X, SUMMARY, HEAD_DIM)
    far = max(Y // 2, 1)
    scratch = [
        pltpu.SMEM((1,), jnp.int32),
        pltpu.VMEM((rows, width), BF16),
        pltpu.VMEM((rows, width), BF16),
        pltpu.VMEM((rows, width), BF16),
        pltpu.VMEM((N, width, width), BF16),
        pltpu.VMEM((N, rows, width), BF16),
        pltpu.VMEM((rows, width), F32),
        pltpu.VMEM(table, BF16),
        pltpu.VMEM(across, BF16),
        pltpu.VMEM((heads, slots, HEAD_DIM), BF16),
        pltpu.VMEM((rows, width), BF16),
        pltpu.VMEM((rows, 2 * width), BF16),
        pltpu.VMEM((heads, rows, rows), F32),
        pltpu.VMEM((heads, rows, rows), F32),
        pltpu.VMEM((heads, rows, rows), BF16),
        pltpu.VMEM((heads, rows, rows), BF16),
        pltpu.VMEM((heads, rows, slots), BF16),
        pltpu.VMEM((Y, width, width), BF16),
        pltpu.VMEM((Y, rows, width), BF16),
        pltpu.VMEM((2 * CHUNKS, far, rows // CHUNKS, width), BF16),
        pltpu.VMEM(table, BF16),
        pltpu.VMEM(across, BF16),
        pltpu.VMEM((heads, X, Z, SUMMARY, HEAD_DIM), BF16),
        pltpu.VMEM((heads, Z, X, SUMMARY, HEAD_DIM), BF16),
        pltpu.VMEM((heads, Z, SUMMARY, HEAD_DIM), BF16),
        pltpu.VMEM((heads, X, SUMMARY, HEAD_DIM), BF16),
        pltpu.VMEM((Z, heads, SUMMARY, HEAD_DIM), BF16),
        pltpu.VMEM((X, heads, SUMMARY, HEAD_DIM), BF16),
        pltpu.VMEM((heads, rows, HEAD_DIM), F32),
        pltpu.VMEM((heads, rows, HEAD_DIM), F32),
        pltpu.SemaphoreType.DMA((2, N)),
        pltpu.SemaphoreType.DMA((4,)),
        pltpu.SemaphoreType.DMA((4 + 4 * heads, max(X, Z))),
        pltpu.SemaphoreType.DMA((4 + 4 * heads, max(X, Z))),
        pltpu.SemaphoreType.DMA((Y + heads,)),
        pltpu.SemaphoreType.DMA((Y + heads,)),
        pltpu.SemaphoreType.DMA((2 * CHUNKS, far)),
        pltpu.SemaphoreType.DMA((2 * CHUNKS, far)),
    ]
    held = pltpu.VMEM((rows, width), BF16)
    results = pl.pallas_call(
        functools.partial(kernel, sizes),
        out_shape=(held, held, held, held),
        in_specs=[hbm] * 6,
        out_specs=(vmem, vmem, vmem, vmem),
        scratch_shapes=scratch,
        compiler_params=pltpu.CompilerParams(collective_id=0, has_side_effects=True),
        name="sparse_attention_step",
    )(summary_index, queries, key_rows, value_rows, out_weight, out_grad)
    return tuple(pl.pallas_call(
        store,
        out_shape=(out, out, out, out),
        in_specs=[vmem] * 4,
        out_specs=(hbm,) * 4,
        scratch_shapes=[pltpu.SemaphoreType.DMA((4,))],
        name="store_results",
    )(*[pltpu.with_memory_space_constraint(r, pltpu.VMEM) for r in results]))


def solution(mesh, sizes=SIZES):
    return jax.shard_map(
        functools.partial(on_device, sizes),
        mesh=mesh,
        in_specs=(
            P("ctx", "head"),
            P("ctx", "head"),
            P("ctx", "head"),
            P("ctx"),
            P("head", None),
            P("ctx", None),
        ),
        out_specs=(P("ctx", "head"), P("ctx", "head"), P("ctx", "head"), P("ctx", "head")),
        check_vma=False,
    )
```
